512 devices in a mesh: tm: 16 (over z), expert: 32 (over x, y, core).
Axes of the slice: x: 4, y: 4, z: 16, core: 2. Of those that a mesh axis runs over, the one named last changes fastest.
Arguments:
- x_in: float32 [32, 4096, 1024], P('expert', 'tm'), may hold values from -6 to 6
- z_gate: bfloat16 [32, 4096, 1024], P('expert', 'tm'), may hold values from -6 to 6
- b_proj: float32 [32, 4096, 128], P('expert', 'tm'), may hold values from -1.5 to 1.5
- c_proj: float32 [32, 4096, 128], P('expert', 'tm'), may hold values from -1.5 to 1.5
- decay_log: float32 [32, 4096, 16], P('expert', 'tm'), as said below
- skip_gain: float32 [16], replicated, may hold values from 0.5 to 2
- residual: float32 [32, 4096, 1024], P('expert', 'tm'), may hold values from -6 to 6
- ssd_gain: float32 [1024], replicated, may hold values from 0.5 to 1.5
- moe_gain: float32 [1024], replicated, may hold values from 0.5 to 1.5
- w_gate: bfloat16 [32, 1024, 1536], P('expert', 'tm'), may hold values from -0.1875 to 0.1875
- w_up: bfloat16 [32, 1024, 1536], P('expert', 'tm'), may hold values from -0.1875 to 0.1875
- w_down: bfloat16 [32, 1536, 1024], P('expert', 'tm'), may hold values from -0.15625 to 0.15625
- routes: int32 [32, 4096, 2], P('expert', 'tm'), may hold values from 0 to 31, all different within a row; in each aligned block of 256 rows (0 to 255, 256 to 511, ..., all dimensions but the last counted through in order) at most 24 rows name the same one
- route_weights: float32 [32, 4096, 2], P('expert', 'tm'), may hold values from 0.2 to 1
Outputs:
- mixed: float32 [32, 4096, 1024], P('expert', 'tm')
The draws below stay inside these ranges and needn't reach their ends.
Inputs may be any that keep to these rules, and one draw needn't show every extreme that they name: `routes`: the two experts of a time step differ. Among the time steps of one device no expert is named more than 24 times, and in every draw some device names some expert exactly 24 times. `decay_log`: every entry is at most zero.
All inputs are finite; a program needn't handle non-finite values.
Results may differ from the reference program's by a relative error of at most 0.0021.
Values may be sent and summed in bfloat16 or wider, within the bound.
No kernel may reach another device: no remote copies, remote signals or barrier semaphores. Data moves between devices by JAX's collectives and lax.ppermute only.
A program may use at most 64 MiB of HBM per device.

```python
import math
import jax
import jax.numpy as jnp
import numpy as np
from jax import lax

D = 1024
HEADS = 16
STATE = 128
FF = 1536
L_DEV = 256
SEQ = 4096
SEQS = 32
EXPERTS = 32
CAP = 24


def draw_decay_log(key, part):
    keys = jax.random.split(key, 7)
    cutoff = 5
    quick = jax.random.randint(keys[0], (HEADS,), 0, 10) < cutoff
    quick_rate = jnp.exp(jax.random.uniform(keys[1], (HEADS,), jnp.float32, math.log(1.0 / 50.0), math.log(1.0 / 30.0)))
    slow_rate = jnp.exp(jax.random.uniform(keys[2], (HEADS,), jnp.float32, math.log(0.1), math.log(0.5))) / SEQ
    rates = jnp.where(quick, quick_rate, slow_rate)
    blocks = SEQ // L_DEV
    block_factor = jnp.exp(jax.random.uniform(keys[3], (SEQS, blocks, 1, HEADS), jnp.float32, math.log(0.5), math.log(2.0)))
    block_factor = jnp.broadcast_to(block_factor, (SEQS, blocks, L_DEV, HEADS)).reshape(SEQS, SEQ, HEADS)
    step_factor = jnp.exp(jax.random.uniform(keys[4], (SEQS, SEQ, HEADS), jnp.float32, math.log(0.5), math.log(2.0)))
    spots = jax.random.randint(keys[5], (SEQS, 3), 0, SEQ)
    places = jnp.any(jnp.arange(SEQ)[None, None, :] == spots[:, :, None], axis=1)
    losses = jnp.log(jax.random.uniform(keys[6], (SEQS, SEQ, HEADS), jnp.float32, 0.5, 0.8))
    return -rates[None, None, :] * block_factor * step_factor + jnp.where(places[:, :, None], losses, 0.0)


def block_levels(rng, shape, shards, least, largest):
    factor_of, own = 1.0, jax.random.fold_in(rng, 6)
    for dim, shards_of in shards:
        heights = jnp.exp(jax.random.uniform(jax.random.fold_in(own, dim), (shards_of,), jnp.float32, least / len(shards), largest / len(shards)))
        factor_of = factor_of * jnp.repeat(heights, shape[dim] // shards_of).reshape([-1 if axis == dim else 1 for axis in range(len(shape))])
    return factor_of


def routed_block(rng, own, number, rows, amount, top, most, lean):
    ranking = jax.random.permutation(rng, amount)
    heavy_load, usual = shares(amount, rows * top, most, lean, True), shares(amount, rows * top, most, lean, False)
    places = jnp.arange(amount)

    def named(sizes, offset_by):
        used = int((sizes > 0).sum())
        fixed = max(1, used // 4)
        moved = fixed + (places - fixed + offset_by * (used - fixed)) % max(1, amount - fixed)
        return jnp.zeros((amount,), jnp.int32).at[ranking[jnp.where(places < fixed, places, moved)]].set(jnp.asarray(sizes, jnp.int32))

    sizes = jnp.where(number % 4 == 0, named(heavy_load, number // 4), named(usual, number - number // 4 - 1))
    mixed = jax.random.permutation(jax.random.fold_in(own, 3), amount)
    donor, receiver = mixed[0:amount // 2 * 2:2], mixed[1:amount // 2 * 2:2]
    slack = jnp.minimum(sizes[donor] - 1, most - sizes[receiver]) // 2
    slack = jnp.where((donor == ranking[0]) | (receiver == ranking[0]) | (sizes[receiver] == 0), 0, jnp.maximum(slack, 0))
    moved = jax.random.randint(jax.random.fold_in(own, 4), (amount // 2,), 0, 1 << 20) % (slack + 1)
    sizes = sizes.at[donor].add(-moved).at[receiver].add(moved)
    members = jnp.searchsorted(jnp.cumsum(sizes), jnp.arange(rows * top), side="right").astype(jnp.int32)
    grid = members.reshape(top, rows).T
    grid = grid[jax.random.permutation(jax.random.fold_in(own, 1), rows)]
    offset_by = jax.random.randint(jax.random.fold_in(own, 2), (rows, 1), 0, top)
    return jnp.take_along_axis(grid, (jnp.arange(top)[None, :] + offset_by) % top, axis=1)


def shares(count, total, limit, skew, full):
    weights = [(1 << 20) // math.isqrt(standing ** skew) + 1 for standing in range(1, count + 1)]
    largest = limit if full else min(limit, max(-(-total // count), total * weights[0] // sum(weights)))
    least = 1 if total - largest >= count - 1 else 0
    counts, rest = [largest] + [least] * (count - 1), total - largest - least * (count - 1)
    while rest > 0:
        movable = [i for i in range(1, count) if counts[i] < largest] or [i for i in range(1, count) if counts[i] < limit]
        mass, remaining = sum([weights[i] for i in movable]), rest
        for i in movable:
            more = min(limit - counts[i], max(1, remaining * weights[i] // mass), rest)
            counts[i] = counts[i] + more
            rest = rest - more
    return np.array(counts)


def gaussian(stream_key, dims, deviation, most, cuts=(), held_as=jnp.bfloat16):
    entries = deviation * jax.random.normal(stream_key, dims, jnp.float32)
    if cuts:
        entries = entries * block_levels(stream_key, dims, cuts, -0.22, 0.18)
    return jnp.clip(entries, -most, most).astype(held_as)


def setup_inputs(seed: int = 0) -> dict:
    arg_keys = jax.random.split(jax.random.key(seed), 15)
    x_in = gaussian(arg_keys[0], (SEQS, SEQ, D), 1.0, 6.0, ((0, 32), (1, 16)), jnp.float32)
    z_gate = gaussian(arg_keys[1], (SEQS, SEQ, D), 1.0, 6.0, ((0, 32), (1, 16)))
    b_proj = gaussian(arg_keys[2], (SEQS, SEQ, STATE), 0.25, 1.5, ((0, 32), (1, 16)), jnp.float32)
    c_proj = gaussian(arg_keys[3], (SEQS, SEQ, STATE), 0.25, 1.5, ((0, 32), (1, 16)), jnp.float32)
    decay_log = draw_decay_log(jax.random.fold_in(arg_keys[14], 71), 0)
    skip_gain = jnp.clip(jnp.exp(jax.random.uniform(arg_keys[5], (HEADS,), jnp.float32, math.log(0.5), math.log(2.0))), 0.5, 2.0)
    residual = gaussian(arg_keys[6], (SEQS, SEQ, D), 1.0, 6.0, ((0, 32), (1, 16)), jnp.float32)
    ssd_gain = jnp.clip(1.0 + 0.1 * jax.random.normal(arg_keys[7], (D,), jnp.float32), 0.5, 1.5)
    moe_gain = jnp.clip(1.0 + 0.1 * jax.random.normal(arg_keys[8], (D,), jnp.float32), 0.5, 1.5)
    w_gate = gaussian(arg_keys[9], (EXPERTS, D, FF), D ** -0.5, 0.1875, ((0, 32), (1, 16)))
    w_up = gaussian(arg_keys[10], (EXPERTS, D, FF), D ** -0.5, 0.1875, ((0, 32), (1, 16)))
    w_down = gaussian(arg_keys[11], (EXPERTS, FF, D), FF ** -0.5, 0.15625, ((0, 32), (1, 16)))
    routes_keys = jax.random.split(jax.random.fold_in(arg_keys[12], 1), SEQS * SEQ // L_DEV)
    routes_turns = jax.random.permutation(jax.random.fold_in(arg_keys[12], 3), SEQS * SEQ // L_DEV)
    routes = jax.vmap(lambda own, number: routed_block(jax.random.fold_in(arg_keys[12], 2), own, number, L_DEV, EXPERTS, 2, CAP, 2))(routes_keys, routes_turns).reshape((SEQS, SEQ, 2))
    route_weights = jnp.clip(0.2 + 0.8 * jax.random.uniform(arg_keys[13], (SEQS, SEQ, 2), jnp.float32) ** block_levels(arg_keys[13], (SEQS, SEQ, 2), ((0, 32), (1, 16)), -0.2, 0.2), 0.2, 1.0)
    return dict(x_in=x_in, z_gate=z_gate, b_proj=b_proj, c_proj=c_proj, decay_log=decay_log, skip_gain=skip_gain, residual=residual, ssd_gain=ssd_gain, moe_gain=moe_gain, w_gate=w_gate, w_up=w_up, w_down=w_down, routes=routes, route_weights=route_weights)


exact_mode = lax.Precision.HIGHEST

def group_carry(state, values, b_rows, running):
    remains = jnp.exp(running[-1][None, :] - running)
    fresh = jnp.einsum('jhp,jn->hpn', values * remains[:, :, None], b_rows, precision=exact_mode)
    return jnp.exp(running[-1])[:, None, None] * state + fresh

def group_step(state, inputs, skip_gain):
    values, b_rows, c_rows, log_rates = inputs
    length = values.shape[0]
    running = jnp.cumsum(log_rates, axis=0)
    across = running.T[:, :, None] - running.T[:, None, :]
    places = jnp.arange(length)
    causal = (places[:, None] >= places[None, :])[None]
    masked = jnp.where(causal, jnp.exp(jnp.where(causal, across, 0.0)), 0.0)
    scores = jnp.dot(c_rows, b_rows.T, precision=exact_mode)
    mixing = masked * scores[None]
    output = jnp.einsum('hij,jhp->ihp', mixing, values, precision=exact_mode)
    output = output + jnp.exp(running)[:, :, None] * jnp.einsum('in,hpn->ihp', c_rows, state, precision=exact_mode)
    output = output + skip_gain[None, :, None] * values
    return (group_carry(state, values, b_rows, running), output)

def sequence_scan(values, b_rows, c_rows, log_rates, skip_gain):
    length, heads, width = values.shape
    block = math.gcd(length, 256)
    count = length // block
    inputs = (values.reshape(count, block, heads, width), b_rows.reshape(count, block, -1), c_rows.reshape(count, block, -1), log_rates.reshape(count, block, heads))
    start = jnp.zeros((heads, width, b_rows.shape[1]), jnp.float32)
    _, outputs = lax.scan(lambda state, piece: group_step(state, piece, skip_gain), start, inputs)
    return outputs.reshape(length, heads * width)

def rms_scale(rows, gain):
    return gain * rows / jnp.sqrt(lax.optimization_barrier(jnp.mean(rows * rows, axis=-1, keepdims=True)) + 1e-05)

def expert_apply(rows, gate_mat, up_mat, down_mat):
    gate = jnp.dot(rows, gate_mat, preferred_element_type=jnp.float32)
    upper = jnp.dot(rows, up_mat, preferred_element_type=jnp.float32)
    hidden = (jax.nn.silu(gate) * upper).astype(jnp.bfloat16)
    return jnp.dot(hidden, down_mat, preferred_element_type=jnp.float32).astype(jnp.bfloat16)

def reference(x_in, z_gate, b_proj, c_proj, decay_log, skip_gain, residual, ssd_gain, moe_gain, w_gate, w_up, w_down, routes, route_weights):
    heads = skip_gain.shape[0]
    width = D // heads

    def one_sequence(item):
        return sequence_scan(item[0].reshape(SEQ, heads, width), item[1], item[2], item[3], skip_gain)
    mixed_ssd = lax.map(one_sequence, (x_in, b_proj, c_proj, decay_log))
    gated = mixed_ssd * jax.nn.silu(z_gate.astype(jnp.float32))
    hres = residual + rms_scale(gated, ssd_gain)
    normed = rms_scale(hres, moe_gain).astype(jnp.bfloat16)
    total = SEQS * SEQ
    flat_rows = normed.reshape(total, D)
    flat_routes = routes.reshape(total, 2)
    flat_weights = route_weights.reshape(total, 2)
    bound = min(total, total // L_DEV * CAP)

    def one_expert(index, accum):
        chosen = flat_routes == index
        member = jnp.any(chosen, axis=1)
        scale = lax.optimization_barrier(jnp.sum(jnp.where(chosen, flat_weights, 0.0), axis=1))
        picks = jnp.nonzero(member, size=bound, fill_value=0)[0]
        live = jnp.arange(bound) < jnp.sum(member.astype(jnp.int32))
        result = expert_apply(flat_rows[picks], w_gate[index], w_up[index], w_down[index]).astype(jnp.float32)
        result = result * jnp.where(live, scale[picks], 0.0)[:, None]
        return accum.at[picks].add(result)
    moe = lax.fori_loop(0, EXPERTS, one_expert, jnp.zeros((total, D), jnp.float32))
    return hres + moe.reshape(SEQS, SEQ, D)
```

```python
import jax
import jax.numpy as jnp
from jax import lax
from jax.experimental import pallas as pl
from jax.experimental.pallas import tpu as pltpu
from jax.sharding import PartitionSpec as P

exact_mode = lax.Precision.HIGHEST
bf16 = jnp.bfloat16
f32 = jnp.float32
MIB = 1 << 20

f16 = jnp.float16
HEAD_PAD = 8
SPLIT = 2048.0
FF_BLOCK = 512
OUT_BLOCK = 512


def rms_scale(rows, gain):
    return gain * rows / jnp.sqrt(jnp.mean(rows * rows, axis=-1, keepdims=True) + 1e-05)


def pack_weights(gate, up, down):
    moves, row = [], 0
    for which, piece, step in ((0, gate, FF_BLOCK), (1, up, FF_BLOCK), (2, down, OUT_BLOCK)):
        for column in range(0, piece.shape[1], step):
            moves.append((which, column, row, piece.shape[0]))
            row += piece.shape[0]

    def body(gate_ref, up_ref, down_ref, out_ref, sems):
        sources = (gate_ref, up_ref, down_ref)
        copies = [
            pltpu.make_async_copy(
                sources[which].at[:, column : column + FF_BLOCK],
                out_ref.at[first : first + rows, :],
                sems.at[i],
            )
            for i, (which, column, first, rows) in enumerate(moves)
        ]
        for copy in copies:
            copy.start()
        for copy in copies:
            copy.wait()

    anywhere = pl.BlockSpec(memory_space=pl.ANY)
    return pl.pallas_call(
        body,
        in_specs=[anywhere] * 3,
        out_specs=anywhere,
        out_shape=jax.ShapeDtypeStruct((row, FF_BLOCK), gate.dtype),
        scratch_shapes=[pltpu.SemaphoreType.DMA((len(moves),))],
    )(gate, up, down)


def scan_states(received):
    count, padded, state = received.shape
    width = padded - HEAD_PAD

    def body(in_ref, out_ref):
        running = jnp.zeros((width, state), f32)
        for z in range(count):
            out_ref[z] = running.astype(out_ref.dtype)
            if z + 1 < count:
                tail = in_ref[z, width:padded, :].astype(f32)
                decay = tail[0:1, :] + (tail[1:2, :] + tail[2:3, :] / SPLIT) / SPLIT
                running = decay * running + in_ref[z, 0:width, :].astype(f32)

    return pl.pallas_call(
        body, out_shape=jax.ShapeDtypeStruct((count, width, state), received.dtype)
    )(received)


def expert_layer(rows, weights, model_width, hidden_width):
    total = rows.shape[0]
    parts = weights.shape[0]
    k_rows = model_width // parts
    f_rows = hidden_width // parts
    ff_steps = hidden_width // FF_BLOCK
    out_steps = model_width // OUT_BLOCK
    down_first = (2 * ff_steps * k_rows) // f_rows
    row_block = 256

    def body(x_ref, g_ref, u_ref, d_ref, out_ref, hid_ref):
        step = pl.program_id(0)
        for f in range(ff_steps):

            @pl.when(step == f)
            def _(f=f):
                wg = g_ref[...].reshape(model_width, FF_BLOCK)
                wu = u_ref[...].reshape(model_width, FF_BLOCK)
                for r in range(0, total, row_block):
                    x = x_ref[r : r + row_block, :]
                    gate = jnp.dot(x, wg, preferred_element_type=f32)
                    upper = jnp.dot(x, wu, preferred_element_type=f32)
                    hidden = (gate / (1.0 + jnp.exp(-gate))) * upper
                    hid_ref[r : r + row_block, f * FF_BLOCK : (f + 1) * FF_BLOCK] = hidden.astype(bf16)

        @pl.when(step >= ff_steps)
        def _():
            wd = d_ref[...].reshape(hidden_width, OUT_BLOCK)
            for r in range(0, total, row_block):
                out_ref[r : r + row_block, :] = jnp.dot(
                    hid_ref[r : r + row_block, :], wd, preferred_element_type=f32
                ).astype(bf16)

    last = ff_steps - 1
    return pl.pallas_call(
        body,
        grid=(ff_steps + out_steps,),
        in_specs=[
            pl.BlockSpec((total, model_width), lambda i: (0, 0)),
            pl.BlockSpec((parts, k_rows, FF_BLOCK), lambda i: (0, jnp.minimum(i, last), 0)),
            pl.BlockSpec((parts, k_rows, FF_BLOCK), lambda i: (0, ff_steps + jnp.minimum(i, last), 0)),
            pl.BlockSpec(
                (parts, f_rows, OUT_BLOCK),
                lambda i: (0, down_first + jnp.maximum(i - ff_steps, 0), 0),
            ),
        ],
        out_specs=pl.BlockSpec((total, OUT_BLOCK), lambda i: (0, jnp.maximum(i - ff_steps, 0))),
        out_shape=jax.ShapeDtypeStruct((total, model_width), bf16),
        scratch_shapes=[pltpu.VMEM((total, hidden_width), bf16)],
        compiler_params=pltpu.CompilerParams(vmem_limit_bytes=40 * MIB),
    )(rows, *[pltpu.with_memory_space_constraint(weights, pltpu.HBM)] * 3)


def combine(back, hres, targets, route_weights):
    slots, model_width = back.shape
    length = hres.shape[0]
    block = 256

    def body(back_ref, hres_ref, target_ref, weight_ref, out_ref, sel_ref):
        @pl.when(pl.program_id(0) == 0)
        def _():
            places = lax.broadcasted_iota(jnp.int32, (length, slots), 1)
            for k in range(2):
                sel_ref[k] = jnp.where(target_ref[:, k : k + 1] == places, 1.0, 0.0).astype(bf16)

        back_block = back_ref[...]
        first = jnp.dot(sel_ref[0], back_block, preferred_element_type=f32)
        second = jnp.dot(sel_ref[1], back_block, preferred_element_type=f32)
        out_ref[...] = hres_ref[...] + (weight_ref[:, 0:1] * first + weight_ref[:, 1:2] * second)

    return pl.pallas_call(
        body,
        grid=(model_width // block,),
        in_specs=[
            pl.BlockSpec((slots, block), lambda i: (0, i)),
            pl.BlockSpec((length, block), lambda i: (0, i)),
            pl.BlockSpec((length, 2), lambda i: (0, 0)),
            pl.BlockSpec((length, 2), lambda i: (0, 0)),
        ],
        out_specs=pl.BlockSpec((length, block), lambda i: (0, i)),
        out_shape=jax.ShapeDtypeStruct((length, model_width), f32),
        scratch_shapes=[pltpu.VMEM((2, length, slots), bf16)],
        compiler_params=pltpu.CompilerParams(vmem_limit_bytes=32 * MIB),
    )(back, hres, targets, route_weights)


def per_device(
    x_in,
    z_gate,
    b_proj,
    c_proj,
    decay_log,
    skip_gain,
    residual,
    ssd_gain,
    moe_gain,
    w_gate,
    w_up,
    w_down,
    routes,
    route_weights,
):
    heads = skip_gain.shape[0]
    length, model_width = x_in.shape[1], x_in.shape[2]
    width = model_width // heads
    hidden_width = w_gate.shape[2]
    experts = lax.axis_size("expert")
    capacity = max(2, 3 * length // experts)

    gathered = lax.all_gather(pack_weights(w_gate[0], w_up[0], w_down[0]), "tm", axis=0)

    values = x_in[0].reshape(length, heads, width)
    b_rows = b_proj[0]
    c_rows = c_proj[0]
    running = jnp.cumsum(decay_log[0], axis=0)

    remains = jnp.exp(running[-1][None, :] - running)
    local_end = jnp.einsum("jhp,jn->hpn", values * remains[:, :, None], b_rows, precision=exact_mode)
    through = jnp.exp(running[-1])
    part_a = lax.reduce_precision(through, 5, 10)
    rest = (through - part_a) * SPLIT
    part_b = lax.reduce_precision(rest, 5, 10)
    part_c = (rest - part_b) * SPLIT
    zero = jnp.zeros_like(through)
    tail = jnp.stack([part_a, part_b, part_c] + [zero] * (HEAD_PAD - 3), axis=1)
    tail = jnp.broadcast_to(tail[:, :, None], (heads, HEAD_PAD, b_rows.shape[1]))
    outgoing_state = jnp.concatenate([local_end, tail], axis=1).astype(f16)
    by_head = lax.all_to_all(outgoing_state, "tm", 0, 0, tiled=True).astype(f32)
    incoming = lax.all_to_all(scan_states(by_head).astype(f16), "tm", 0, 0, tiled=True).astype(f32)

    across = running.T[:, :, None] - running.T[:, None, :]
    places = jnp.arange(length)
    causal = (places[:, None] >= places[None, :])[None]
    masked = jnp.where(causal, jnp.exp(jnp.where(causal, across, 0.0)), 0.0)
    scores = jnp.dot(c_rows, b_rows.T, precision=exact_mode)
    inside = jnp.einsum("hij,jhp->ihp", masked * scores[None], values, precision=exact_mode)
    inside = inside + skip_gain[None, :, None] * values

    carried = jnp.exp(running)[:, :, None] * jnp.einsum(
        "in,hpn->ihp", c_rows, incoming, precision=exact_mode
    )
    mixed_ssd = (inside + carried).reshape(length, model_width)
    gated = mixed_ssd * jax.nn.silu(z_gate[0].astype(f32))
    hres = residual[0] + rms_scale(gated, ssd_gain)
    normed = rms_scale(hres, moe_gain).astype(bf16)

    chosen = routes[0]
    expert_ids = jnp.arange(experts)
    hit = (chosen[:, 0:1] == expert_ids) | (chosen[:, 1:2] == expert_ids)
    before = (places[:, None] > places[None, :]).astype(bf16)
    rank = jnp.dot(before, hit.astype(bf16), preferred_element_type=f32).astype(jnp.int32)
    slot = jnp.sum(
        jnp.where(chosen[:, :, None] == expert_ids[None, None, :], rank[:, None, :], 0), axis=2
    )
    targets = chosen * capacity + slot
    slot_ids = jnp.arange(experts * capacity)
    spread = (
        (targets[:, 0][None, :] == slot_ids[:, None]) | (targets[:, 1][None, :] == slot_ids[:, None])
    ).astype(bf16)
    outgoing = jnp.dot(spread, normed, preferred_element_type=f32).astype(bf16)
    received = lax.all_to_all(
        outgoing.reshape(experts, capacity, model_width), "expert", 0, 0, tiled=True
    )
    produced = expert_layer(
        received.reshape(experts * capacity, model_width), gathered, model_width, hidden_width
    )
    back = lax.all_to_all(
        produced.reshape(experts, capacity, model_width), "expert", 0, 0, tiled=True
    )
    out = combine(back.reshape(experts * capacity, model_width), hres, targets, route_weights[0])
    return out.reshape(1, length, model_width)


def solution(mesh):
    split = P("expert", "tm", None)
    in_specs = (split,) * 5 + (P(), split, P(), P()) + (split,) * 5
    return jax.shard_map(
        per_device, mesh=mesh, in_specs=in_specs, out_specs=split, check_vma=False
    )
```

```python
import jax
import jax.numpy as jnp
from jax import lax
from jax.experimental import pallas as pl
from jax.experimental.pallas import tpu as pltpu
from jax.sharding import PartitionSpec as P

exact_mode = lax.Precision.HIGHEST
bf16 = jnp.bfloat16
f32 = jnp.float32
MIB = 1 << 20

f16 = jnp.float16
HEAD_PAD = 8
SPLIT = 2048.0
FF_BLOCK = 512
OUT_BLOCK = 512


def rms_scale(rows, gain):
    return gain * rows / jnp.sqrt(jnp.mean(rows * rows, axis=-1, keepdims=True) + 1e-05)


def pack_weights(gate, up, down):
    moves, row = [], 0
    for which, piece in enumerate((gate, up, down)):
        for column in range(0, piece.shape[1], FF_BLOCK):
            moves.append((which, column, row, piece.shape[0]))
            row += piece.shape[0]

    def body(gate_ref, up_ref, down_ref, out_ref):
        sources = (gate_ref, up_ref, down_ref)
        for which, column, first, rows in moves:
            out_ref[first : first + rows, :] = sources[which][:, column : column + FF_BLOCK]

    return pl.pallas_call(body, out_shape=jax.ShapeDtypeStruct((row, FF_BLOCK), gate.dtype))(
        gate, up, down
    )


def incoming_states(local_end, through):
    heads, width, state = local_end.shape
    count = lax.axis_size("tm")
    group = 4
    groups = [[g * group + m for m in range(group)] for g in range(count // group)]
    part_a = lax.reduce_precision(through, 5, 10)
    rest = (through - part_a) * SPLIT
    part_b = lax.reduce_precision(rest, 5, 10)
    part_c = (rest - part_b) * SPLIT
    zero = jnp.zeros_like(through)
    tail = jnp.stack([part_a, part_b, part_c] + [zero] * (HEAD_PAD - 3), axis=1)
    tail = jnp.broadcast_to(tail[:, :, None], (heads, HEAD_PAD, state))
    sent = jnp.concatenate([local_end, tail], axis=1).astype(f16)
    shared = lax.all_to_all(sent, "tm", 0, 0, tiled=True, axis_index_groups=groups)
    shared = shared.reshape(group, heads // group, width + HEAD_PAD, state).astype(f32)
    own = shared[:, :, :width]
    tail = shared[:, :, width:]
    decay = tail[:, :, 0:1] + (tail[:, :, 1:2] + tail[:, :, 2:3] / SPLIT) / SPLIT

    total, passed = own[0], decay[0]
    for m in range(1, group):
        total = decay[m] * total + own[m]
        passed = passed * decay[m]
    entry = jnp.zeros_like(total)
    for g in range(count // group - 1):
        hops = [(g * group + m, (g + 1) * group + m) for m in range(group)]
        handed = lax.ppermute((passed * entry + total).astype(f16), "tm", hops)
        entry = entry + handed.astype(f32)
    before = [entry]
    for m in range(group - 1):
        before.append(decay[m] * before[-1] + own[m])
    returned = jnp.concatenate(before, axis=0).astype(f16)
    return lax.all_to_all(returned, "tm", 0, 0, tiled=True, axis_index_groups=groups).astype(f32)


def expert_layer(rows, weights, model_width, hidden_width):
    total = rows.shape[0]
    parts = weights.shape[0]
    k_rows = model_width // parts
    f_rows = hidden_width // parts
    ff_steps = hidden_width // FF_BLOCK
    out_steps = model_width // OUT_BLOCK
    down_first = (2 * ff_steps * k_rows) // f_rows
    row_block = 256

    def body(x_ref, g_ref, u_ref, d_ref, out_ref, hid_ref):
        step = pl.program_id(0)
        for f in range(ff_steps):

            @pl.when(step == f)
            def _(f=f):
                wg = g_ref[...].reshape(model_width, FF_BLOCK)
                wu = u_ref[...].reshape(model_width, FF_BLOCK)
                for r in range(0, total, row_block):
                    x = x_ref[r : r + row_block, :]
                    gate = jnp.dot(x, wg, preferred_element_type=f32)
                    upper = jnp.dot(x, wu, preferred_element_type=f32)
                    hidden = (gate / (1.0 + jnp.exp(-gate))) * upper
                    hid_ref[r : r + row_block, f * FF_BLOCK : (f + 1) * FF_BLOCK] = hidden.astype(bf16)

        @pl.when(step >= ff_steps)
        def _():
            wd = d_ref[...].reshape(hidden_width, OUT_BLOCK)
            for r in range(0, total, row_block):
                out_ref[r : r + row_block, :] = jnp.dot(
                    hid_ref[r : r + row_block, :], wd, preferred_element_type=f32
                ).astype(bf16)

    last = ff_steps - 1
    return pl.pallas_call(
        body,
        grid=(ff_steps + out_steps,),
        in_specs=[
            pl.BlockSpec((total, model_width), lambda i: (0, 0)),
            pl.BlockSpec((parts, k_rows, FF_BLOCK), lambda i: (0, jnp.minimum(i, last), 0)),
            pl.BlockSpec((parts, k_rows, FF_BLOCK), lambda i: (0, ff_steps + jnp.minimum(i, last), 0)),
            pl.BlockSpec(
                (parts, f_rows, OUT_BLOCK),
                lambda i: (0, down_first + jnp.maximum(i - ff_steps, 0), 0),
            ),
        ],
        out_specs=pl.BlockSpec((total, OUT_BLOCK), lambda i: (0, jnp.maximum(i - ff_steps, 0))),
        out_shape=jax.ShapeDtypeStruct((total, model_width), bf16),
        scratch_shapes=[pltpu.VMEM((total, hidden_width), bf16)],
        compiler_params=pltpu.CompilerParams(vmem_limit_bytes=40 * MIB),
    )(rows, *[pltpu.with_memory_space_constraint(weights, pltpu.HBM)] * 3)


def combine(back, hres, targets, route_weights):
    slots, model_width = back.shape
    length = hres.shape[0]
    block = 256

    def body(back_ref, hres_ref, target_ref, weight_ref, out_ref, sel_ref):
        @pl.when(pl.program_id(0) == 0)
        def _():
            places = lax.broadcasted_iota(jnp.int32, (length, slots), 1)
            for k in range(2):
                sel_ref[k] = jnp.where(target_ref[:, k : k + 1] == places, 1.0, 0.0).astype(bf16)

        back_block = back_ref[...]
        first = jnp.dot(sel_ref[0], back_block, preferred_element_type=f32)
        second = jnp.dot(sel_ref[1], back_block, preferred_element_type=f32)
        out_ref[...] = hres_ref[...] + (weight_ref[:, 0:1] * first + weight_ref[:, 1:2] * second)

    return pl.pallas_call(
        body,
        grid=(model_width // block,),
        in_specs=[
            pl.BlockSpec((slots, block), lambda i: (0, i)),
            pl.BlockSpec((length, block), lambda i: (0, i)),
            pl.BlockSpec((length, 2), lambda i: (0, 0)),
            pl.BlockSpec((length, 2), lambda i: (0, 0)),
        ],
        out_specs=pl.BlockSpec((length, block), lambda i: (0, i)),
        out_shape=jax.ShapeDtypeStruct((length, model_width), f32),
        scratch_shapes=[pltpu.VMEM((2, length, slots), bf16)],
        compiler_params=pltpu.CompilerParams(vmem_limit_bytes=32 * MIB),
    )(back, hres, targets, route_weights)


def per_device(
    x_in,
    z_gate,
    b_proj,
    c_proj,
    decay_log,
    skip_gain,
    residual,
    ssd_gain,
    moe_gain,
    w_gate,
    w_up,
    w_down,
    routes,
    route_weights,
):
    heads = skip_gain.shape[0]
    length, model_width = x_in.shape[1], x_in.shape[2]
    width = model_width // heads
    hidden_width = w_gate.shape[2]
    experts = lax.axis_size("expert")
    capacity = max(2, 3 * length // experts)

    gathered = lax.all_gather(pack_weights(w_gate[0], w_up[0], w_down[0]), "tm", axis=0)

    values = x_in[0].reshape(length, heads, width)
    b_rows = b_proj[0]
    c_rows = c_proj[0]
    running = jnp.cumsum(decay_log[0], axis=0)

    remains = jnp.exp(running[-1][None, :] - running)
    local_end = jnp.einsum("jhp,jn->hpn", values * remains[:, :, None], b_rows, precision=exact_mode)
    through = jnp.exp(running[-1])
    incoming = incoming_states(local_end, through)

    across = running.T[:, :, None] - running.T[:, None, :]
    places = jnp.arange(length)
    causal = (places[:, None] >= places[None, :])[None]
    masked = jnp.where(causal, jnp.exp(jnp.where(causal, across, 0.0)), 0.0)
    scores = jnp.dot(c_rows, b_rows.T, precision=exact_mode)
    inside = jnp.einsum("hij,jhp->ihp", masked * scores[None], values, precision=exact_mode)
    inside = inside + skip_gain[None, :, None] * values

    carried = jnp.exp(running)[:, :, None] * jnp.einsum(
        "in,hpn->ihp", c_rows, incoming, precision=exact_mode
    )
    mixed_ssd = (inside + carried).reshape(length, model_width)
    gated = mixed_ssd * jax.nn.silu(z_gate[0].astype(f32))
    hres = residual[0] + rms_scale(gated, ssd_gain)
    normed = rms_scale(hres, moe_gain).astype(bf16)

    chosen = routes[0]
    expert_ids = jnp.arange(experts)
    hit = (chosen[:, 0:1] == expert_ids) | (chosen[:, 1:2] == expert_ids)
    before = (places[:, None] > places[None, :]).astype(bf16)
    rank = jnp.dot(before, hit.astype(bf16), preferred_element_type=f32).astype(jnp.int32)
    slot = jnp.sum(
        jnp.where(chosen[:, :, None] == expert_ids[None, None, :], rank[:, None, :], 0), axis=2
    )
    targets = chosen * capacity + slot
    slot_ids = jnp.arange(experts * capacity)
    spread = (
        (targets[:, 0][None, :] == slot_ids[:, None]) | (targets[:, 1][None, :] == slot_ids[:, None])
    ).astype(bf16)
    outgoing = jnp.dot(spread, normed, preferred_element_type=f32).astype(bf16)
    received = lax.all_to_all(
        outgoing.reshape(experts, capacity, model_width), "expert", 0, 0, tiled=True
    )
    produced = expert_layer(
        received.reshape(experts * capacity, model_width), gathered, model_width, hidden_width
    )
    back = lax.all_to_all(
        produced.reshape(experts, capacity, model_width), "expert", 0, 0, tiled=True
    )
    out = combine(back.reshape(experts * capacity, model_width), hres, targets, route_weights[0])
    return out.reshape(1, length, model_width)


def solution(mesh):
    split = P("expert", "tm", None)
    in_specs = (split,) * 5 + (P(), split, P(), P()) + (split,) * 5
    return jax.shard_map(
        per_device, mesh=mesh, in_specs=in_specs, out_specs=split, check_vma=False
    )
```

```python
import jax
import jax.numpy as jnp
from jax import lax
from jax.experimental import pallas as pl
from jax.experimental.pallas import tpu as pltpu
from jax.sharding import PartitionSpec as P

exact_mode = lax.Precision.HIGHEST
bf16 = jnp.bfloat16
f32 = jnp.float32
MIB = 1 << 20

f16 = jnp.float16
HEAD_PAD = 8
SPLIT = 2048.0
FF_BLOCK = 512


def rms_scale(rows, gain):
    return gain * rows / jnp.sqrt(jnp.mean(rows * rows, axis=-1, keepdims=True) + 1e-05)


def pack_weights(gate, up, down):
    moves, row = [], 0
    for which, piece in enumerate((gate, up, down)):
        for column in range(0, piece.shape[1], FF_BLOCK):
            moves.append((which, column, row, piece.shape[0]))
            row += piece.shape[0]

    def body(gate_ref, up_ref, down_ref, out_ref):
        sources = (gate_ref, up_ref, down_ref)
        for which, column, first, rows in moves:
            out_ref[first : first + rows, :] = sources[which][:, column : column + FF_BLOCK]

    return pl.pallas_call(body, out_shape=jax.ShapeDtypeStruct((row, FF_BLOCK), gate.dtype))(
        gate, up, down
    )


def incoming_states(local_end, through):
    heads, width, state = local_end.shape
    count = lax.axis_size("tm")
    group = 4
    groups = [[g * group + m for m in range(group)] for g in range(count // group)]
    part_a = lax.reduce_precision(through, 5, 10)
    rest = (through - part_a) * SPLIT
    part_b = lax.reduce_precision(rest, 5, 10)
    part_c = (rest - part_b) * SPLIT
    zero = jnp.zeros_like(through)
    tail = jnp.stack([part_a, part_b, part_c] + [zero] * (HEAD_PAD - 3), axis=1)
    tail = jnp.broadcast_to(tail[:, :, None], (heads, HEAD_PAD, state))
    sent = jnp.concatenate([local_end, tail], axis=1).astype(f16)
    shared = lax.all_to_all(sent, "tm", 0, 0, tiled=True, axis_index_groups=groups)
    shared = shared.reshape(group, heads // group, width + HEAD_PAD, state).astype(f32)
    own = shared[:, :, :width]
    tail = shared[:, :, width:]
    decay = tail[:, :, 0:1] + (tail[:, :, 1:2] + tail[:, :, 2:3] / SPLIT) / SPLIT

    total, passed = own[0], decay[0]
    for m in range(1, group):
        total = decay[m] * total + own[m]
        passed = passed * decay[m]
    entry = jnp.zeros_like(total)
    for g in range(count // group - 1):
        hops = [(g * group + m, (g + 1) * group + m) for m in range(group)]
        handed = lax.ppermute((passed * entry + total).astype(f16), "tm", hops)
        entry = entry + handed.astype(f32)
    before = [entry]
    for m in range(group - 1):
        before.append(decay[m] * before[-1] + own[m])
    returned = jnp.concatenate(before, axis=0).astype(f16)
    return lax.all_to_all(returned, "tm", 0, 0, tiled=True, axis_index_groups=groups).astype(f32)


def expert_layer(rows, weights, model_width, hidden_width):
    total = rows.shape[0]
    parts, packed, _ = weights.shape
    k_rows = model_width // parts
    f_rows = hidden_width // parts
    ff_steps = hidden_width // FF_BLOCK
    out_steps = model_width // FF_BLOCK
    blocks = [(k_rows * i, k_rows) for i in range(2 * ff_steps)]
    blocks += [(2 * ff_steps * k_rows + f_rows * i, f_rows) for i in range(out_steps)]
    down = list(range(2 * ff_steps, len(blocks)))
    order = [b for f in range(ff_steps) for b in (f, ff_steps + f)] + down
    out_rows = total // 3

    def body(x_ref, w_ref, out_ref, w_buf, hid_ref, out_buf, w_sems, out_sems):
        def copy(block, part):
            first, count = blocks[block]
            return pltpu.make_async_copy(
                w_ref.at[part, first : first + count, :],
                w_buf.at[part, first : first + count, :],
                w_sems.at[block, part],
            )

        for block in order:
            for part in range(parts):
                copy(block, part).start()

        def matrix(block):
            first, count = blocks[block]
            for part in range(parts):
                copy(block, part).wait()
            return w_buf[:, first : first + count, :].reshape(parts * count, FF_BLOCK)

        for f in range(ff_steps):
            x = x_ref[...]
            gate = jnp.dot(x, matrix(f), preferred_element_type=f32)
            upper = jnp.dot(x, matrix(ff_steps + f), preferred_element_type=f32)
            hidden = (gate / (1.0 + jnp.exp(-gate))) * upper
            hid_ref[:, f * FF_BLOCK : (f + 1) * FF_BLOCK] = hidden.astype(bf16)
        sides = [matrix(block) for block in down]
        leaving = []
        for i, r in enumerate(range(0, total, out_rows)):
            for n, side in enumerate(sides):
                out_buf[r : r + out_rows, n * FF_BLOCK : (n + 1) * FF_BLOCK] = jnp.dot(
                    hid_ref[r : r + out_rows, :], side, preferred_element_type=f32
                ).astype(bf16)
            leaving.append(
                pltpu.make_async_copy(
                    out_buf.at[r : r + out_rows, :], out_ref.at[r : r + out_rows, :], out_sems.at[i]
                )
            )
            leaving[-1].start()
        for each in leaving:
            each.wait()

    anywhere = pl.BlockSpec(memory_space=pl.ANY)
    return pl.pallas_call(
        body,
        in_specs=[pl.BlockSpec(memory_space=pltpu.VMEM), anywhere],
        out_specs=anywhere,
        out_shape=jax.ShapeDtypeStruct((total, model_width), bf16),
        scratch_shapes=[
            pltpu.VMEM((parts, packed, FF_BLOCK), bf16),
            pltpu.VMEM((total, hidden_width), bf16),
            pltpu.VMEM((total, model_width), bf16),
            pltpu.SemaphoreType.DMA((len(blocks), parts)),
            pltpu.SemaphoreType.DMA((3,)),
        ],
        compiler_params=pltpu.CompilerParams(vmem_limit_bytes=32 * MIB),
    )(rows, pltpu.with_memory_space_constraint(weights, pltpu.HBM))


def combine(back, hres, selection, route_weights):
    length, model_width = hres.shape
    block = 256
    steps = model_width // block

    def body(back_ref, hres_ref, sel_ref, weight_in, out_ref, out_buf, weight_ref, sems):
        arriving = pltpu.make_async_copy(weight_in, weight_ref, sems.at[steps])
        arriving.start()
        leaving = []
        for i in range(steps):
            part = slice(i * block, (i + 1) * block)
            rows = back_ref[:, part]
            first = jnp.dot(sel_ref[0], rows, preferred_element_type=f32)
            second = jnp.dot(sel_ref[1], rows, preferred_element_type=f32)
            if i == 0:
                arriving.wait()
                weight_a, weight_b = weight_ref[:, 0:1], weight_ref[:, 1:2]
            out_buf[:, part] = hres_ref[:, part] + (weight_a * first + weight_b * second)
            leaving.append(
                pltpu.make_async_copy(out_buf.at[:, part], out_ref.at[:, part], sems.at[i])
            )
            leaving[-1].start()
        for each in leaving:
            each.wait()

    return pl.pallas_call(
        body,
        in_specs=[pl.BlockSpec(memory_space=pltpu.VMEM)] * 3 + [pl.BlockSpec(memory_space=pl.ANY)],
        out_specs=pl.BlockSpec(memory_space=pl.ANY),
        out_shape=jax.ShapeDtypeStruct((length, model_width), f32),
        scratch_shapes=[
            pltpu.VMEM((length, model_width), f32),
            pltpu.VMEM(route_weights.shape, f32),
            pltpu.SemaphoreType.DMA((steps + 1,)),
        ],
        compiler_params=pltpu.CompilerParams(vmem_limit_bytes=16 * MIB),
    )(back, hres, selection, route_weights)


def per_device(
    x_in,
    z_gate,
    b_proj,
    c_proj,
    decay_log,
    skip_gain,
    residual,
    ssd_gain,
    moe_gain,
    w_gate,
    w_up,
    w_down,
    routes,
    route_weights,
):
    heads = skip_gain.shape[0]
    length, model_width = x_in.shape[1], x_in.shape[2]
    width = model_width // heads
    hidden_width = w_gate.shape[2]
    experts = lax.axis_size("expert")
    capacity = max(2, 3 * length // experts)

    gathered = lax.all_gather(pack_weights(w_gate[0], w_up[0], w_down[0]), "tm", axis=0)

    values = x_in[0].reshape(length, heads, width)
    b_rows = b_proj[0]
    c_rows = c_proj[0]
    running = jnp.cumsum(decay_log[0], axis=0)

    remains = jnp.exp(running[-1][None, :] - running)
    local_end = jnp.einsum("jhp,jn->hpn", values * remains[:, :, None], b_rows, precision=exact_mode)
    through = jnp.exp(running[-1])
    incoming = incoming_states(local_end, through)

    across = running.T[:, :, None] - running.T[:, None, :]
    places = jnp.arange(length)
    causal = (places[:, None] >= places[None, :])[None]
    masked = jnp.where(causal, jnp.exp(jnp.where(causal, across, 0.0)), 0.0)
    scores = jnp.dot(c_rows, b_rows.T, precision=exact_mode)
    inside = jnp.einsum("hij,jhp->ihp", masked * scores[None], values, precision=exact_mode)
    inside = inside + skip_gain[None, :, None] * values

    carried = jnp.exp(running)[:, :, None] * jnp.einsum(
        "in,hpn->ihp", c_rows, incoming, precision=exact_mode
    )
    mixed_ssd = (inside + carried).reshape(length, model_width)
    gated = mixed_ssd * jax.nn.silu(z_gate[0].astype(f32))
    hres = residual[0] + rms_scale(gated, ssd_gain)
    normed = rms_scale(hres, moe_gain).astype(bf16)

    chosen = routes[0]
    expert_ids = jnp.arange(experts)
    hit = (chosen[:, 0:1] == expert_ids) | (chosen[:, 1:2] == expert_ids)
    before = (places[:, None] > places[None, :]).astype(bf16)
    rank = jnp.dot(before, hit.astype(bf16), preferred_element_type=f32).astype(jnp.int32)
    slot = jnp.sum(
        jnp.where(chosen[:, :, None] == expert_ids[None, None, :], rank[:, None, :], 0), axis=2
    )
    targets = chosen * capacity + slot
    slot_ids = jnp.arange(experts * capacity)
    spread = (
        (targets[:, 0][None, :] == slot_ids[:, None]) | (targets[:, 1][None, :] == slot_ids[:, None])
    ).astype(bf16)
    selection = jnp.stack(
        [targets[:, k : k + 1] == slot_ids[None, :] for k in range(targets.shape[1])]
    ).astype(bf16)
    outgoing = jnp.dot(spread, normed, preferred_element_type=f32).astype(bf16)
    received = lax.all_to_all(
        outgoing.reshape(experts, capacity, model_width), "expert", 0, 0, tiled=True
    )
    produced = expert_layer(
        received.reshape(experts * capacity, model_width), gathered, model_width, hidden_width
    )
    back = lax.all_to_all(
        produced.reshape(experts, capacity, model_width), "expert", 0, 0, tiled=True
    )
    out = combine(back.reshape(experts * capacity, model_width), hres, selection, route_weights[0])
    return out.reshape(1, length, model_width)


def solution(mesh):
    split = P("expert", "tm", None)
    in_specs = (split,) * 5 + (P(), split, P(), P()) + (split,) * 5
    return jax.shard_map(
        per_device, mesh=mesh, in_specs=in_specs, out_specs=split, check_vma=False
    )
```

```python
import jax
import jax.numpy as jnp
from jax import lax
from jax.experimental import pallas as pl
from jax.experimental.pallas import tpu as pltpu
from jax.sharding import PartitionSpec as P

exact_mode = lax.Precision.HIGHEST
bf16 = jnp.bfloat16
f32 = jnp.float32
MIB = 1 << 20

f16 = jnp.float16
HEAD_PAD = 8
SPLIT = 2048.0
FF_BLOCK = 512


def rms_scale(rows, gain):
    return gain * rows / jnp.sqrt(jnp.mean(rows * rows, axis=-1, keepdims=True) + 1e-05)


def pack_weights(gate, up, down):
    moves, row = [], 0
    for which, piece in enumerate((gate, up, down)):
        for column in range(0, piece.shape[1], FF_BLOCK):
            moves.append((which, column, row, piece.shape[0]))
            row += piece.shape[0]

    def body(gate_ref, up_ref, down_ref, out_ref):
        sources = (gate_ref, up_ref, down_ref)
        for which, column, first, rows in moves:
            out_ref[first : first + rows, :] = sources[which][:, column : column + FF_BLOCK]

    return pl.pallas_call(body, out_shape=jax.ShapeDtypeStruct((row, FF_BLOCK), gate.dtype))(
        gate, up, down
    )


def incoming_states(local_end, through):
    heads, width, state = local_end.shape
    count = lax.axis_size("tm")
    group = 4
    groups = [[g * group + m for m in range(group)] for g in range(count // group)]
    part_a = lax.reduce_precision(through, 5, 10)
    rest = (through - part_a) * SPLIT
    part_b = lax.reduce_precision(rest, 5, 10)
    part_c = (rest - part_b) * SPLIT
    zero = jnp.zeros_like(through)
    tail = jnp.stack([part_a, part_b, part_c] + [zero] * (HEAD_PAD - 3), axis=1)
    tail = jnp.broadcast_to(tail[:, :, None], (heads, HEAD_PAD, state))
    sent = jnp.concatenate([local_end, tail], axis=1).astype(f16)
    shared = lax.all_to_all(sent, "tm", 0, 0, tiled=True, axis_index_groups=groups)
    shared = shared.reshape(group, heads // group, width + HEAD_PAD, state).astype(f32)
    own = shared[:, :, :width]
    tail = shared[:, :, width:]
    decay = tail[:, :, 0:1] + (tail[:, :, 1:2] + tail[:, :, 2:3] / SPLIT) / SPLIT

    total, passed = own[0], decay[0]
    for m in range(1, group):
        total = decay[m] * total + own[m]
        passed = passed * decay[m]
    entry = jnp.zeros_like(total)
    for g in range(count // group - 1):
        hops = [(g * group + m, (g + 1) * group + m) for m in range(group)]
        handed = lax.ppermute((passed * entry + total).astype(f16), "tm", hops)
        entry = entry + handed.astype(f32)
    before = [entry]
    for m in range(group - 1):
        before.append(decay[m] * before[-1] + own[m])
    returned = jnp.concatenate(before, axis=0).astype(f16)
    return lax.all_to_all(returned, "tm", 0, 0, tiled=True, axis_index_groups=groups).astype(f32)


def expert_layer(rows, weights, model_width, hidden_width):
    total = rows.shape[0]
    parts, packed, _ = weights.shape
    k_rows = model_width // parts
    f_rows = hidden_width // parts
    ff_steps = hidden_width // FF_BLOCK
    out_steps = model_width // FF_BLOCK
    blocks = [(k_rows * i, k_rows) for i in range(2 * ff_steps)]
    blocks += [(2 * ff_steps * k_rows + f_rows * i, f_rows) for i in range(out_steps)]
    down = list(range(2 * ff_steps, len(blocks)))
    order = [b for f in range(ff_steps) for b in (f, ff_steps + f)] + down
    out_rows = total // 3

    def body(x_ref, w_ref, out_ref, w_buf, hid_ref, out_buf, w_sems, out_sems):
        def copy(block):
            first, count = blocks[block]
            return pltpu.make_async_copy(
                w_ref.at[:, first : first + count, :],
                w_buf.at[:, first : first + count, :],
                w_sems.at[block],
            )

        for block in order:
            copy(block).start()

        def matrix(block):
            first, count = blocks[block]
            copy(block).wait()
            return w_buf[:, first : first + count, :].reshape(parts * count, FF_BLOCK)

        for f in range(ff_steps):
            w_gate, w_up = matrix(f), matrix(ff_steps + f)
            gate = jnp.dot(x_ref[...], w_gate, preferred_element_type=f32)
            upper = jnp.dot(x_ref[...], w_up, preferred_element_type=f32)
            hidden = (gate / (1.0 + jnp.exp(-gate))) * upper
            hid_ref[:, f * FF_BLOCK : (f + 1) * FF_BLOCK] = hidden.astype(bf16)
        sides = [matrix(block) for block in down]
        leaving = []
        for i, r in enumerate(range(0, total, out_rows)):
            for n, side in enumerate(sides):
                out_buf[r : r + out_rows, n * FF_BLOCK : (n + 1) * FF_BLOCK] = jnp.dot(
                    hid_ref[r : r + out_rows, :], side, preferred_element_type=f32
                ).astype(bf16)
            leaving.append(
                pltpu.make_async_copy(
                    out_buf.at[r : r + out_rows, :], out_ref.at[r : r + out_rows, :], out_sems.at[i]
                )
            )
            leaving[-1].start()
        for each in leaving:
            each.wait()

    anywhere = pl.BlockSpec(memory_space=pl.ANY)
    return pl.pallas_call(
        body,
        in_specs=[pl.BlockSpec(memory_space=pltpu.VMEM), anywhere],
        out_specs=anywhere,
        out_shape=jax.ShapeDtypeStruct((total, model_width), bf16),
        scratch_shapes=[
            pltpu.VMEM((parts, packed, FF_BLOCK), bf16),
            pltpu.VMEM((total, hidden_width), bf16),
            pltpu.VMEM((total, model_width), bf16),
            pltpu.SemaphoreType.DMA((len(blocks),)),
            pltpu.SemaphoreType.DMA((3,)),
        ],
        compiler_params=pltpu.CompilerParams(vmem_limit_bytes=32 * MIB),
    )(rows, pltpu.with_memory_space_constraint(weights, pltpu.HBM))


def combine(back, hres, selection):
    length, model_width = hres.shape
    block = 256
    steps = model_width // block

    def body(back_ref, hres_ref, sel_ref, out_ref, out_buf, sems):
        leaving = []
        for i in range(steps):
            part = slice(i * block, (i + 1) * block)
            rows = back_ref[:, part]
            first = jnp.dot(sel_ref[0], rows, preferred_element_type=f32)
            second = jnp.dot(sel_ref[1], rows, preferred_element_type=f32)
            out_buf[:, part] = hres_ref[:, part] + (first + second)
            leaving.append(
                pltpu.make_async_copy(out_buf.at[:, part], out_ref.at[:, part], sems.at[i])
            )
            leaving[-1].start()
        for each in leaving:
            each.wait()

    return pl.pallas_call(
        body,
        in_specs=[pl.BlockSpec(memory_space=pltpu.VMEM)] * 3,
        out_specs=pl.BlockSpec(memory_space=pl.ANY),
        out_shape=jax.ShapeDtypeStruct((length, model_width), f32),
        scratch_shapes=[pltpu.VMEM((length, model_width), f32), pltpu.SemaphoreType.DMA((steps,))],
        compiler_params=pltpu.CompilerParams(vmem_limit_bytes=16 * MIB),
    )(back, hres, selection)


def per_device(
    x_in,
    z_gate,
    b_proj,
    c_proj,
    decay_log,
    skip_gain,
    residual,
    ssd_gain,
    moe_gain,
    w_gate,
    w_up,
    w_down,
    routes,
    route_weights,
):
    heads = skip_gain.shape[0]
    length, model_width = x_in.shape[1], x_in.shape[2]
    width = model_width // heads
    hidden_width = w_gate.shape[2]
    experts = lax.axis_size("expert")
    capacity = max(2, 3 * length // experts)

    gathered = lax.all_gather(pack_weights(w_gate[0], w_up[0], w_down[0]), "tm", axis=0)

    values = x_in[0].reshape(length, heads, width)
    b_rows = b_proj[0]
    c_rows = c_proj[0]
    running = jnp.cumsum(decay_log[0], axis=0)

    remains = jnp.exp(running[-1][None, :] - running)
    local_end = jnp.einsum("jhp,jn->hpn", values * remains[:, :, None], b_rows, precision=exact_mode)
    through = jnp.exp(running[-1])
    incoming = incoming_states(local_end, through)

    across = running.T[:, :, None] - running.T[:, None, :]
    places = jnp.arange(length)
    causal = (places[:, None] >= places[None, :])[None]
    masked = jnp.where(causal, jnp.exp(jnp.where(causal, across, 0.0)), 0.0)
    scores = jnp.dot(c_rows, b_rows.T, precision=exact_mode)
    inside = jnp.einsum("hij,jhp->ihp", masked * scores[None], values, precision=exact_mode)
    inside = inside + skip_gain[None, :, None] * values

    carried = jnp.exp(running)[:, :, None] * jnp.einsum(
        "in,hpn->ihp", c_rows, incoming, precision=exact_mode
    )
    mixed_ssd = (inside + carried).reshape(length, model_width)
    gated = mixed_ssd * jax.nn.silu(z_gate[0].astype(f32))
    hres = residual[0] + rms_scale(gated, ssd_gain)
    normed = rms_scale(hres, moe_gain).astype(bf16)

    chosen = routes[0]
    expert_ids = jnp.arange(experts)
    hit = (chosen[:, 0:1] == expert_ids) | (chosen[:, 1:2] == expert_ids)
    before = (places[:, None] > places[None, :]).astype(bf16)
    rank = jnp.dot(before, hit.astype(bf16), preferred_element_type=f32).astype(jnp.int32)
    slot = jnp.sum(
        jnp.where(chosen[:, :, None] == expert_ids[None, None, :], rank[:, None, :], 0), axis=2
    )
    targets = chosen * capacity + slot
    slot_ids = jnp.arange(experts * capacity)
    spread = (
        (targets[:, 0][None, :] == slot_ids[:, None]) | (targets[:, 1][None, :] == slot_ids[:, None])
    ).astype(bf16)
    weights = route_weights[0]
    leading = lax.reduce_precision(weights, 8, 7)
    selection = jnp.stack(
        [
            sum(
                jnp.where(targets[:, k : k + 1] == slot_ids[None, :], half[:, k : k + 1], 0.0)
                for k in range(targets.shape[1])
            )
            for half in (leading, weights - leading)
        ]
    ).astype(bf16)
    outgoing = jnp.dot(spread, normed, preferred_element_type=f32).astype(bf16)
    received = lax.all_to_all(
        outgoing.reshape(experts, capacity, model_width), "expert", 0, 0, tiled=True
    )
    produced = expert_layer(
        received.reshape(experts * capacity, model_width), gathered, model_width, hidden_width
    )
    back = lax.all_to_all(
        produced.reshape(experts, capacity, model_width), "expert", 0, 0, tiled=True
    )
    out = combine(back.reshape(experts * capacity, model_width), hres, selection)
    return out.reshape(1, length, model_width)


def solution(mesh):
    split = P("expert", "tm", None)
    in_specs = (split,) * 5 + (P(), split, P(), P()) + (split,) * 5
    return jax.shard_map(
        per_device, mesh=mesh, in_specs=in_specs, out_specs=split, check_vma=False
    )
```

```python
import jax
import jax.numpy as jnp
from jax import lax
from jax.experimental import pallas as pl
from jax.experimental.pallas import tpu as pltpu
from jax.sharding import PartitionSpec as P

exact_mode = lax.Precision.HIGHEST
bf16 = jnp.bfloat16
f32 = jnp.float32
MIB = 1 << 20

f16 = jnp.float16
HEAD_PAD = 8
SPLIT = 2048.0
FF_BLOCK = 512


def rms_scale(rows, gain):
    return gain * rows / jnp.sqrt(jnp.mean(rows * rows, axis=-1, keepdims=True) + 1e-05)


def pack_weights(gate, up, down):
    moves, row = [], 0
    for which, piece in enumerate((gate, up, down)):
        for column in range(0, piece.shape[1], FF_BLOCK):
            moves.append((which, column, row, piece.shape[0]))
            row += piece.shape[0]

    def body(gate_ref, up_ref, down_ref, out_ref):
        sources = (gate_ref, up_ref, down_ref)
        for which, column, first, rows in moves:
            out_ref[first : first + rows, :] = sources[which][:, column : column + FF_BLOCK]

    return pl.pallas_call(body, out_shape=jax.ShapeDtypeStruct((row, FF_BLOCK), gate.dtype))(
        gate, up, down
    )


def incoming_states(local_end, through):
    heads, width, state = local_end.shape
    count = lax.axis_size("tm")
    group = 4
    groups = [[g * group + m for m in range(group)] for g in range(count // group)]
    part_a = lax.reduce_precision(through, 5, 10)
    rest = (through - part_a) * SPLIT
    part_b = lax.reduce_precision(rest, 5, 10)
    part_c = (rest - part_b) * SPLIT
    zero = jnp.zeros_like(through)
    tail = jnp.stack([part_a, part_b, part_c] + [zero] * (HEAD_PAD - 3), axis=1)
    tail = jnp.broadcast_to(tail[:, :, None], (heads, HEAD_PAD, state))
    sent = jnp.concatenate([local_end, tail], axis=1).astype(f16)
    shared = lax.all_to_all(sent, "tm", 0, 0, tiled=True, axis_index_groups=groups)
    shared = shared.reshape(group, heads // group, width + HEAD_PAD, state).astype(f32)
    own = shared[:, :, :width]
    tail = shared[:, :, width:]
    decay = tail[:, :, 0:1] + (tail[:, :, 1:2] + tail[:, :, 2:3] / SPLIT) / SPLIT

    total, passed = own[0], decay[0]
    for m in range(1, group):
        total = decay[m] * total + own[m]
        passed = passed * decay[m]
    entry = jnp.zeros_like(total)
    for g in range(count // group - 1):
        hops = [(g * group + m, (g + 1) * group + m) for m in range(group)]
        handed = lax.ppermute((passed * entry + total).astype(f16), "tm", hops)
        entry = entry + handed.astype(f32)
    before = [entry]
    for m in range(group - 1):
        before.append(decay[m] * before[-1] + own[m])
    returned = jnp.concatenate(before, axis=0).astype(f16)
    return lax.all_to_all(returned, "tm", 0, 0, tiled=True, axis_index_groups=groups).astype(f32)


def expert_layer(rows, weights, model_width, hidden_width):
    total = rows.shape[0]
    parts, packed, _ = weights.shape
    k_rows = model_width // parts
    f_rows = hidden_width // parts
    ff_steps = hidden_width // FF_BLOCK
    out_steps = model_width // FF_BLOCK
    gates = [(k_rows * i, k_rows, 0, FF_BLOCK) for i in range(2 * ff_steps)]
    downs = [(2 * ff_steps * k_rows + f_rows * i, f_rows, 0, FF_BLOCK) for i in range(out_steps)]
    half = FF_BLOCK // 2
    pairs = [
        ((0, k_rows, at, half), (ff_steps * k_rows, k_rows, at, half), at) for at in (0, half)
    ]
    pairs += [(gates[f], gates[ff_steps + f], f * FF_BLOCK) for f in range(1, ff_steps)]
    order = [block for pair in pairs for block in pair[:2]] + downs

    def body(x_ref, w_ref, out_ref, w_buf, hid_ref, sems):
        def copy(block):
            first, rows, at, columns = block
            place = (slice(None), slice(first, first + rows), slice(at, at + columns))
            return pltpu.make_async_copy(w_ref.at[place], w_buf.at[place], sems.at[order.index(block)])

        for block in order:
            copy(block).start()

        def matrix(block):
            first, rows, at, columns = block
            copy(block).wait()
            return w_buf[:, first : first + rows, at : at + columns].reshape(parts * rows, columns)

        for gate_block, up_block, at in pairs:
            w_gate, w_up = matrix(gate_block), matrix(up_block)
            gate = jnp.dot(x_ref[...], w_gate, preferred_element_type=f32)
            upper = jnp.dot(x_ref[...], w_up, preferred_element_type=f32)
            hidden = (gate / (1.0 + jnp.exp(-gate))) * upper
            hid_ref[:, at : at + gate_block[3]] = hidden.astype(bf16)
        for n, block in enumerate(downs):
            out_ref[:, n * FF_BLOCK : (n + 1) * FF_BLOCK] = jnp.dot(
                hid_ref[...], matrix(block), preferred_element_type=f32
            ).astype(bf16)

    in_vmem = pl.BlockSpec(memory_space=pltpu.VMEM)
    return pl.pallas_call(
        body,
        in_specs=[in_vmem, pl.BlockSpec(memory_space=pl.ANY)],
        out_specs=in_vmem,
        out_shape=pltpu.VMEM((total, model_width), bf16),
        scratch_shapes=[
            pltpu.VMEM((parts, packed, FF_BLOCK), bf16),
            pltpu.VMEM((total, hidden_width), bf16),
            pltpu.SemaphoreType.DMA((len(order),)),
        ],
        compiler_params=pltpu.CompilerParams(vmem_limit_bytes=32 * MIB),
    )(rows, pltpu.with_memory_space_constraint(weights, pltpu.HBM))


def combine(back, hres, selection):
    length, model_width = hres.shape
    block = 256
    steps = model_width // block

    def body(back_ref, hres_ref, sel_ref, out_ref, out_buf, sems):
        leaving = []
        for i in range(steps):
            part = slice(i * block, (i + 1) * block)
            rows = back_ref[:, part]
            first = jnp.dot(sel_ref[0], rows, preferred_element_type=f32)
            second = jnp.dot(sel_ref[1], rows, preferred_element_type=f32)
            out_buf[:, part] = hres_ref[:, part] + (first + second)
            leaving.append(
                pltpu.make_async_copy(out_buf.at[:, part], out_ref.at[:, part], sems.at[i])
            )
            leaving[-1].start()
        for each in leaving:
            each.wait()

    return pl.pallas_call(
        body,
        in_specs=[pl.BlockSpec(memory_space=pltpu.VMEM)] * 3,
        out_specs=pl.BlockSpec(memory_space=pl.ANY),
        out_shape=jax.ShapeDtypeStruct((length, model_width), f32),
        scratch_shapes=[pltpu.VMEM((length, model_width), f32), pltpu.SemaphoreType.DMA((steps,))],
        compiler_params=pltpu.CompilerParams(vmem_limit_bytes=16 * MIB),
    )(back, hres, selection)


def per_device(
    x_in,
    z_gate,
    b_proj,
    c_proj,
    decay_log,
    skip_gain,
    residual,
    ssd_gain,
    moe_gain,
    w_gate,
    w_up,
    w_down,
    routes,
    route_weights,
):
    heads = skip_gain.shape[0]
    length, model_width = x_in.shape[1], x_in.shape[2]
    width = model_width // heads
    hidden_width = w_gate.shape[2]
    experts = lax.axis_size("expert")
    capacity = max(2, 3 * length // experts)

    gathered = lax.all_gather(pack_weights(w_gate[0], w_up[0], w_down[0]), "tm", axis=0)

    values = x_in[0].reshape(length, heads, width)
    b_rows = b_proj[0]
    c_rows = c_proj[0]
    running = jnp.cumsum(decay_log[0], axis=0)

    remains = jnp.exp(running[-1][None, :] - running)
    local_end = jnp.einsum("jhp,jn->hpn", values * remains[:, :, None], b_rows, precision=exact_mode)
    through = jnp.exp(running[-1])
    incoming = incoming_states(local_end, through)

    across = running.T[:, :, None] - running.T[:, None, :]
    places = jnp.arange(length)
    causal = (places[:, None] >= places[None, :])[None]
    masked = jnp.where(causal, jnp.exp(jnp.where(causal, across, 0.0)), 0.0)
    scores = jnp.dot(c_rows, b_rows.T, precision=exact_mode)
    inside = jnp.einsum("hij,jhp->ihp", masked * scores[None], values, precision=exact_mode)
    inside = inside + skip_gain[None, :, None] * values

    carried = jnp.exp(running)[:, :, None] * jnp.einsum(
        "in,hpn->ihp", c_rows, incoming, precision=exact_mode
    )
    mixed_ssd = (inside + carried).reshape(length, model_width)
    gated = mixed_ssd * jax.nn.silu(z_gate[0].astype(f32))
    hres = residual[0] + rms_scale(gated, ssd_gain)
    normed = rms_scale(hres, moe_gain).astype(bf16)

    chosen = routes[0]
    expert_ids = jnp.arange(experts)
    hit = (chosen[:, 0:1] == expert_ids) | (chosen[:, 1:2] == expert_ids)
    before = (places[:, None] > places[None, :]).astype(bf16)
    rank = jnp.dot(before, hit.astype(bf16), preferred_element_type=f32).astype(jnp.int32)
    slot = jnp.sum(
        jnp.where(chosen[:, :, None] == expert_ids[None, None, :], rank[:, None, :], 0), axis=2
    )
    targets = chosen * capacity + slot
    slot_ids = jnp.arange(experts * capacity)
    spread = (
        (targets[:, 0][None, :] == slot_ids[:, None]) | (targets[:, 1][None, :] == slot_ids[:, None])
    ).astype(bf16)
    weights = route_weights[0]
    leading = lax.reduce_precision(weights, 8, 7)
    selection = jnp.stack(
        [
            sum(
                jnp.where(targets[:, k : k + 1] == slot_ids[None, :], half[:, k : k + 1], 0.0)
                for k in range(targets.shape[1])
            )
            for half in (leading, weights - leading)
        ]
    ).astype(bf16)
    outgoing = jnp.dot(spread, normed, preferred_element_type=f32).astype(bf16)
    received = lax.all_to_all(
        outgoing.reshape(experts, capacity, model_width), "expert", 0, 0, tiled=True
    )
    produced = expert_layer(
        received.reshape(experts * capacity, model_width), gathered, model_width, hidden_width
    )
    back = lax.all_to_all(
        produced.reshape(experts, capacity, model_width), "expert", 0, 0, tiled=True
    )
    out = combine(back.reshape(experts * capacity, model_width), hres, selection)
    return out.reshape(1, length, model_width)


def solution(mesh):
    split = P("expert", "tm", None)
    in_specs = (split,) * 5 + (P(), split, P(), P()) + (split,) * 5
    return jax.shard_map(
        per_device, mesh=mesh, in_specs=in_specs, out_specs=split, check_vma=False
    )
```

```python
import jax
import jax.numpy as jnp
from jax import lax
from jax.experimental import pallas as pl
from jax.experimental.pallas import tpu as pltpu
from jax.sharding import PartitionSpec as P

exact_mode = lax.Precision.HIGHEST
bf16 = jnp.bfloat16
f32 = jnp.float32
MIB = 1 << 20

f16 = jnp.float16
HEAD_PAD = 8
SPLIT = 2048.0
FF_BLOCK = 512


def rms_scale(rows, gain):
    return gain * rows / jnp.sqrt(jnp.mean(rows * rows, axis=-1, keepdims=True) + 1e-05)


def pack_weights(gate, up, down):
    moves, row = [], 0
    for which, piece in enumerate((gate, up, down)):
        for column in range(0, piece.shape[1], FF_BLOCK):
            moves.append((which, column, row, piece.shape[0]))
            row += piece.shape[0]

    def body(gate_ref, up_ref, down_ref, out_ref):
        sources = (gate_ref, up_ref, down_ref)
        for which, column, first, rows in moves:
            out_ref[first : first + rows, :] = sources[which][:, column : column + FF_BLOCK]

    return pl.pallas_call(body, out_shape=jax.ShapeDtypeStruct((row, FF_BLOCK), gate.dtype))(
        gate, up, down
    )


def incoming_states(local_end, through):
    heads, width, state = local_end.shape
    count = lax.axis_size("tm")
    group = 4
    groups = [[g * group + m for m in range(group)] for g in range(count // group)]
    part_a = lax.reduce_precision(through, 5, 10)
    rest = (through - part_a) * SPLIT
    part_b = lax.reduce_precision(rest, 5, 10)
    part_c = (rest - part_b) * SPLIT
    zero = jnp.zeros_like(through)
    tail = jnp.stack([part_a, part_b, part_c] + [zero] * (HEAD_PAD - 3), axis=1)
    tail = jnp.broadcast_to(tail[:, :, None], (heads, HEAD_PAD, state))
    sent = jnp.concatenate([local_end, tail], axis=1).astype(f16)
    shared = lax.all_to_all(sent, "tm", 0, 0, tiled=True, axis_index_groups=groups)
    shared = shared.reshape(group, heads // group, width + HEAD_PAD, state).astype(f32)
    own = shared[:, :, :width]
    tail = shared[:, :, width:]
    decay = tail[:, :, 0:1] + (tail[:, :, 1:2] + tail[:, :, 2:3] / SPLIT) / SPLIT

    total, passed = own[0], decay[0]
    for m in range(1, group):
        total = decay[m] * total + own[m]
        passed = passed * decay[m]
    entry = jnp.zeros_like(total)
    for g in range(count // group - 1):
        hops = [(g * group + m, (g + 1) * group + m) for m in range(group)]
        handed = lax.ppermute((passed * entry + total).astype(f16), "tm", hops)
        entry = entry + handed.astype(f32)
    before = [entry]
    for m in range(group - 1):
        before.append(decay[m] * before[-1] + own[m])
    returned = jnp.concatenate(before, axis=0).astype(f16)
    return lax.all_to_all(returned, "tm", 0, 0, tiled=True, axis_index_groups=groups).astype(f32)


def expert_layer(rows, weights, model_width, hidden_width):
    total = rows.shape[0]
    parts, packed, _ = weights.shape
    k_rows = model_width // parts
    f_rows = hidden_width // parts
    ff_steps = hidden_width // FF_BLOCK
    out_steps = model_width // FF_BLOCK
    blocks = [(k_rows * i, k_rows) for i in range(2 * ff_steps)]
    blocks += [(2 * ff_steps * k_rows + f_rows * i, f_rows) for i in range(out_steps)]
    down = list(range(2 * ff_steps, len(blocks)))
    order = [b for f in range(ff_steps) for b in (f, ff_steps + f)] + down
    out_rows = total // 3

    def body(x_ref, w_ref, out_ref, w_buf, hid_ref, out_buf, w_sems, out_sems):
        def copy(block):
            first, count = blocks[block]
            return pltpu.make_async_copy(
                w_ref.at[:, first : first + count, :],
                w_buf.at[:, first : first + count, :],
                w_sems.at[block],
            )

        for block in order:
            copy(block).start()

        def matrix(block):
            first, count = blocks[block]
            copy(block).wait()
            return w_buf[:, first : first + count, :].reshape(parts * count, FF_BLOCK)

        for f in range(ff_steps):
            w_gate, w_up = matrix(f), matrix(ff_steps + f)
            gate = jnp.dot(x_ref[...], w_gate, preferred_element_type=f32)
            upper = jnp.dot(x_ref[...], w_up, preferred_element_type=f32)
            hidden = (gate / (1.0 + jnp.exp(-gate))) * upper
            hid_ref[:, f * FF_BLOCK : (f + 1) * FF_BLOCK] = hidden.astype(bf16)
        sides = [matrix(block) for block in down]
        leaving = []
        for i, r in enumerate(range(0, total, out_rows)):
            for n, side in enumerate(sides):
                out_buf[r : r + out_rows, n * FF_BLOCK : (n + 1) * FF_BLOCK] = jnp.dot(
                    hid_ref[r : r + out_rows, :], side, preferred_element_type=f32
                ).astype(bf16)
            leaving.append(
                pltpu.make_async_copy(
                    out_buf.at[r : r + out_rows, :], out_ref.at[r : r + out_rows, :], out_sems.at[i]
                )
            )
            leaving[-1].start()
        for each in leaving:
            each.wait()

    anywhere = pl.BlockSpec(memory_space=pl.ANY)
    return pl.pallas_call(
        body,
        in_specs=[pl.BlockSpec(memory_space=pltpu.VMEM), anywhere],
        out_specs=anywhere,
        out_shape=jax.ShapeDtypeStruct((total, model_width), bf16),
        scratch_shapes=[
            pltpu.VMEM((parts, packed, FF_BLOCK), bf16),
            pltpu.VMEM((total, hidden_width), bf16),
            pltpu.VMEM((total, model_width), bf16),
            pltpu.SemaphoreType.DMA((len(blocks),)),
            pltpu.SemaphoreType.DMA((3,)),
        ],
        compiler_params=pltpu.CompilerParams(vmem_limit_bytes=32 * MIB),
    )(rows, pltpu.with_memory_space_constraint(weights, pltpu.HBM))


def combine(back, hres, selection):
    length, model_width = hres.shape
    block = 256
    steps = model_width // block

    def body(back_ref, hres_ref, sel_ref, out_ref, out_buf, sems):
        leaving = []
        for i in range(steps):
            part = slice(i * block, (i + 1) * block)
            rows = back_ref[:, part]
            first = jnp.dot(sel_ref[0], rows, preferred_element_type=f32)
            second = jnp.dot(sel_ref[1], rows, preferred_element_type=f32)
            out_buf[:, part] = hres_ref[:, part] + (first + second)
            leaving.append(
                pltpu.make_async_copy(out_buf.at[:, part], out_ref.at[:, part], sems.at[i])
            )
            leaving[-1].start()
        for each in leaving:
            each.wait()

    return pl.pallas_call(
        body,
        in_specs=[pl.BlockSpec(memory_space=pltpu.VMEM)] * 3,
        out_specs=pl.BlockSpec(memory_space=pl.ANY),
        out_shape=jax.ShapeDtypeStruct((length, model_width), f32),
        scratch_shapes=[pltpu.VMEM((length, model_width), f32), pltpu.SemaphoreType.DMA((steps,))],
        compiler_params=pltpu.CompilerParams(vmem_limit_bytes=16 * MIB),
    )(back, hres, selection)


def per_device(
    x_in,
    z_gate,
    b_proj,
    c_proj,
    decay_log,
    skip_gain,
    residual,
    ssd_gain,
    moe_gain,
    w_gate,
    w_up,
    w_down,
    routes,
    route_weights,
):
    heads = skip_gain.shape[0]
    length, model_width = x_in.shape[1], x_in.shape[2]
    width = model_width // heads
    hidden_width = w_gate.shape[2]
    experts = lax.axis_size("expert")
    capacity = max(2, 3 * length // experts)

    gathered = lax.all_gather(pack_weights(w_gate[0], w_up[0], w_down[0]), "tm", axis=0)

    values = x_in[0].reshape(length, heads, width)
    b_rows = b_proj[0]
    c_rows = c_proj[0]
    running = jnp.cumsum(decay_log[0], axis=0)

    remains = jnp.exp(running[-1][None, :] - running)
    local_end = jnp.einsum("jhp,jn->hpn", values * remains[:, :, None], b_rows, precision=exact_mode)
    through = jnp.exp(running[-1])
    incoming = incoming_states(local_end, through)

    across = running.T[:, :, None] - running.T[:, None, :]
    places = jnp.arange(length)
    causal = (places[:, None] >= places[None, :])[None]
    masked = jnp.where(causal, jnp.exp(jnp.where(causal, across, 0.0)), 0.0)
    scores = jnp.dot(c_rows, b_rows.T, precision=exact_mode)
    inside = jnp.einsum("hij,jhp->ihp", masked * scores[None], values, precision=exact_mode)
    inside = inside + skip_gain[None, :, None] * values

    carried = jnp.exp(running)[:, :, None] * jnp.einsum(
        "in,hpn->ihp", c_rows, incoming, precision=exact_mode
    )
    mixed_ssd = (inside + carried).reshape(length, model_width)
    gated = mixed_ssd * jax.nn.silu(z_gate[0].astype(f32))
    hres = residual[0] + rms_scale(gated, ssd_gain)
    normed = rms_scale(hres, moe_gain).astype(bf16)

    chosen = routes[0]
    expert_ids = jnp.arange(experts)
    hit = (chosen[:, 0:1] == expert_ids) | (chosen[:, 1:2] == expert_ids)
    before = (places[:, None] > places[None, :]).astype(bf16)
    rank = jnp.dot(before, hit.astype(bf16), preferred_element_type=f32).astype(jnp.int32)
    slot = jnp.sum(
        jnp.where(chosen[:, :, None] == expert_ids[None, None, :], rank[:, None, :], 0), axis=2
    )
    targets = chosen * capacity + slot
    slot_ids = jnp.arange(experts * capacity)
    spread = (
        (targets[:, 0][None, :] == slot_ids[:, None]) | (targets[:, 1][None, :] == slot_ids[:, None])
    ).astype(bf16)
    weights = route_weights[0]
    leading = lax.reduce_precision(weights, 8, 7)
    selection = jnp.stack(
        [
            sum(
                jnp.where(targets[:, k : k + 1] == slot_ids[None, :], half[:, k : k + 1], 0.0)
                for k in range(targets.shape[1])
            )
            for half in (leading, weights - leading)
        ]
    ).astype(bf16)
    outgoing = jnp.dot(spread, normed, preferred_element_type=f32).astype(bf16)
    received = lax.all_to_all(
        outgoing.reshape(experts, capacity, model_width), "expert", 0, 0, tiled=True
    )
    received, selection = lax.optimization_barrier((received, selection))
    produced = expert_layer(
        received.reshape(experts * capacity, model_width), gathered, model_width, hidden_width
    )
    back = lax.all_to_all(
        produced.reshape(experts, capacity, model_width), "expert", 0, 0, tiled=True
    )
    out = combine(back.reshape(experts * capacity, model_width), hres, selection)
    return out.reshape(1, length, model_width)


def solution(mesh):
    split = P("expert", "tm", None)
    in_specs = (split,) * 5 + (P(), split, P(), P()) + (split,) * 5
    return jax.shard_map(
        per_device, mesh=mesh, in_specs=in_specs, out_specs=split, check_vma=False
    )
```

```python
import jax
import jax.numpy as jnp
from jax import lax
from jax.experimental import pallas as pl
from jax.experimental.pallas import tpu as pltpu
from jax.sharding import PartitionSpec as P

exact_mode = lax.Precision.HIGHEST
bf16 = jnp.bfloat16
f32 = jnp.float32
MIB = 1 << 20

f16 = jnp.float16
HEAD_PAD = 8
SPLIT = 2048.0
FF_BLOCK = 512


def rms_scale(rows, gain):
    return gain * rows / jnp.sqrt(jnp.mean(rows * rows, axis=-1, keepdims=True) + 1e-05)


def pack_weights(gate, up, down):
    moves, row = [], 0
    for which, piece in enumerate((gate, up, down)):
        for column in range(0, piece.shape[1], FF_BLOCK):
            moves.append((which, column, row, piece.shape[0]))
            row += piece.shape[0]

    def body(gate_ref, up_ref, down_ref, out_ref):
        sources = (gate_ref, up_ref, down_ref)
        for which, column, first, rows in moves:
            out_ref[first : first + rows, :] = sources[which][:, column : column + FF_BLOCK]

    return pl.pallas_call(body, out_shape=jax.ShapeDtypeStruct((row, FF_BLOCK), gate.dtype))(
        gate, up, down
    )


def incoming_states(local_end, through):
    heads, width, state = local_end.shape
    count = lax.axis_size("tm")
    group = 4
    groups = [[g * group + m for m in range(group)] for g in range(count // group)]
    part_a = lax.reduce_precision(through, 5, 10)
    rest = (through - part_a) * SPLIT
    part_b = lax.reduce_precision(rest, 5, 10)
    part_c = (rest - part_b) * SPLIT
    zero = jnp.zeros_like(through)
    tail = jnp.stack([part_a, part_b, part_c] + [zero] * (HEAD_PAD - 3), axis=1)
    tail = jnp.broadcast_to(tail[:, :, None], (heads, HEAD_PAD, state))
    sent = jnp.concatenate([local_end, tail], axis=1).astype(f16)
    shared = lax.all_to_all(sent, "tm", 0, 0, tiled=True, axis_index_groups=groups)
    shared = shared.reshape(group, heads // group, width + HEAD_PAD, state).astype(f32)
    own = shared[:, :, :width]
    tail = shared[:, :, width:]
    decay = tail[:, :, 0:1] + (tail[:, :, 1:2] + tail[:, :, 2:3] / SPLIT) / SPLIT

    total, passed = own[0], decay[0]
    for m in range(1, group):
        total = decay[m] * total + own[m]
        passed = passed * decay[m]
    entry = jnp.zeros_like(total)
    for g in range(count // group - 1):
        hops = [(g * group + m, (g + 1) * group + m) for m in range(group)]
        handed = lax.ppermute((passed * entry + total).astype(f16), "tm", hops)
        entry = entry + handed.astype(f32)
    before = [entry]
    for m in range(group - 1):
        before.append(decay[m] * before[-1] + own[m])
    returned = jnp.concatenate(before, axis=0).astype(f16)
    return lax.all_to_all(returned, "tm", 0, 0, tiled=True, axis_index_groups=groups).astype(f32)


def expert_layer(rows, weights, model_width, hidden_width):
    total = rows.shape[0]
    parts, packed, _ = weights.shape
    k_rows = model_width // parts
    f_rows = hidden_width // parts
    ff_steps = hidden_width // FF_BLOCK
    out_steps = model_width // FF_BLOCK
    gates = [(k_rows * i, k_rows, 0, FF_BLOCK) for i in range(2 * ff_steps)]
    downs = [(2 * ff_steps * k_rows + f_rows * i, f_rows, 0, FF_BLOCK) for i in range(out_steps)]
    half = FF_BLOCK // 2
    pairs = [
        ((0, k_rows, at, half), (ff_steps * k_rows, k_rows, at, half), at) for at in (0, half)
    ]
    pairs += [(gates[f], gates[ff_steps + f], f * FF_BLOCK) for f in range(1, ff_steps)]
    order = [block for pair in pairs for block in pair[:2]] + downs

    def body(x_ref, w_ref, out_ref, w_buf, hid_ref, sems):
        def copy(block):
            first, rows, at, columns = block
            place = (slice(None), slice(first, first + rows), slice(at, at + columns))
            return pltpu.make_async_copy(w_ref.at[place], w_buf.at[place], sems.at[order.index(block)])

        for block in order:
            copy(block).start()

        def matrix(block):
            first, rows, at, columns = block
            copy(block).wait()
            return w_buf[:, first : first + rows, at : at + columns].reshape(parts * rows, columns)

        for gate_block, up_block, at in pairs:
            w_gate, w_up = matrix(gate_block), matrix(up_block)
            gate = jnp.dot(x_ref[...], w_gate, preferred_element_type=f32)
            upper = jnp.dot(x_ref[...], w_up, preferred_element_type=f32)
            hidden = (gate / (1.0 + jnp.exp(-gate))) * upper
            hid_ref[:, at : at + gate_block[3]] = hidden.astype(bf16)
        for n, block in enumerate(downs):
            out_ref[:, n * FF_BLOCK : (n + 1) * FF_BLOCK] = jnp.dot(
                hid_ref[...], matrix(block), preferred_element_type=f32
            ).astype(bf16)

    in_vmem = pl.BlockSpec(memory_space=pltpu.VMEM)
    return pl.pallas_call(
        body,
        in_specs=[in_vmem, pl.BlockSpec(memory_space=pl.ANY)],
        out_specs=in_vmem,
        out_shape=pltpu.VMEM((total, model_width), bf16),
        scratch_shapes=[
            pltpu.VMEM((parts, packed, FF_BLOCK), bf16),
            pltpu.VMEM((total, hidden_width), bf16),
            pltpu.SemaphoreType.DMA((len(order),)),
        ],
        compiler_params=pltpu.CompilerParams(vmem_limit_bytes=32 * MIB),
    )(rows, pltpu.with_memory_space_constraint(weights, pltpu.HBM))


def combine(back, hres, selection):
    length, model_width = hres.shape
    block = 256
    steps = model_width // block

    def body(back_ref, hres_ref, sel_ref, out_ref, out_buf, sems):
        leaving = []
        for i in range(steps):
            part = slice(i * block, (i + 1) * block)
            rows = back_ref[:, part]
            first = jnp.dot(sel_ref[0], rows, preferred_element_type=f32)
            second = jnp.dot(sel_ref[1], rows, preferred_element_type=f32)
            out_buf[:, part] = hres_ref[:, part] + (first + second)
            leaving.append(
                pltpu.make_async_copy(out_buf.at[:, part], out_ref.at[:, part], sems.at[i])
            )
            leaving[-1].start()
        for each in leaving:
            each.wait()

    return pl.pallas_call(
        body,
        in_specs=[pl.BlockSpec(memory_space=pltpu.VMEM)] * 3,
        out_specs=pl.BlockSpec(memory_space=pl.ANY),
        out_shape=jax.ShapeDtypeStruct((length, model_width), f32),
        scratch_shapes=[pltpu.VMEM((length, model_width), f32), pltpu.SemaphoreType.DMA((steps,))],
        compiler_params=pltpu.CompilerParams(vmem_limit_bytes=16 * MIB),
    )(back, hres, selection)


def per_device(
    x_in,
    z_gate,
    b_proj,
    c_proj,
    decay_log,
    skip_gain,
    residual,
    ssd_gain,
    moe_gain,
    w_gate,
    w_up,
    w_down,
    routes,
    route_weights,
):
    heads = skip_gain.shape[0]
    length, model_width = x_in.shape[1], x_in.shape[2]
    width = model_width // heads
    hidden_width = w_gate.shape[2]
    experts = lax.axis_size("expert")
    capacity = max(2, 3 * length // experts)

    gathered = lax.all_gather(pack_weights(w_gate[0], w_up[0], w_down[0]), "tm", axis=0)

    values = x_in[0].reshape(length, heads, width)
    b_rows = b_proj[0]
    c_rows = c_proj[0]
    running = jnp.cumsum(decay_log[0], axis=0)

    remains = jnp.exp(running[-1][None, :] - running)
    local_end = jnp.einsum("jhp,jn->hpn", values * remains[:, :, None], b_rows, precision=exact_mode)
    through = jnp.exp(running[-1])
    incoming = incoming_states(local_end, through)

    across = running.T[:, :, None] - running.T[:, None, :]
    places = jnp.arange(length)
    causal = (places[:, None] >= places[None, :])[None]
    masked = jnp.where(causal, jnp.exp(jnp.where(causal, across, 0.0)), 0.0)
    scores = jnp.dot(c_rows, b_rows.T, precision=exact_mode)
    inside = jnp.einsum("hij,jhp->ihp", masked * scores[None], values, precision=exact_mode)
    inside = inside + skip_gain[None, :, None] * values

    carried = jnp.exp(running)[:, :, None] * jnp.einsum(
        "in,hpn->ihp", c_rows, incoming, precision=exact_mode
    )
    mixed_ssd = (inside + carried).reshape(length, model_width)
    gated = mixed_ssd * jax.nn.silu(z_gate[0].astype(f32))
    hres = residual[0] + rms_scale(gated, ssd_gain)
    normed = rms_scale(hres, moe_gain).astype(bf16)

    chosen = routes[0]
    expert_ids = jnp.arange(experts)
    hit = (chosen[:, 0:1] == expert_ids) | (chosen[:, 1:2] == expert_ids)
    before = (places[:, None] > places[None, :]).astype(bf16)
    rank = jnp.dot(before, hit.astype(bf16), preferred_element_type=f32).astype(jnp.int32)
    slot = jnp.sum(
        jnp.where(chosen[:, :, None] == expert_ids[None, None, :], rank[:, None, :], 0), axis=2
    )
    targets = chosen * capacity + slot
    slot_ids = jnp.arange(experts * capacity)
    spread = (
        (targets[:, 0][None, :] == slot_ids[:, None]) | (targets[:, 1][None, :] == slot_ids[:, None])
    ).astype(bf16)
    weights = route_weights[0]
    leading = lax.reduce_precision(weights, 8, 7)
    selection = jnp.stack(
        [
            sum(
                jnp.where(targets[:, k : k + 1] == slot_ids[None, :], half[:, k : k + 1], 0.0)
                for k in range(targets.shape[1])
            )
            for half in (leading, weights - leading)
        ]
    ).astype(bf16)
    outgoing = jnp.dot(spread, normed, preferred_element_type=f32).astype(bf16)
    received = lax.all_to_all(
        outgoing.reshape(experts, capacity, model_width), "expert", 0, 0, tiled=True
    )
    received, selection = lax.optimization_barrier((received, selection))
    produced = expert_layer(
        received.reshape(experts * capacity, model_width), gathered, model_width, hidden_width
    )
    back = lax.all_to_all(
        produced.reshape(experts, capacity, model_width), "expert", 0, 0, tiled=True
    )
    out = combine(back.reshape(experts * capacity, model_width), hres, selection)
    return out.reshape(1, length, model_width)


def solution(mesh):
    split = P("expert", "tm", None)
    in_specs = (split,) * 5 + (P(), split, P(), P()) + (split,) * 5
    return jax.shard_map(
        per_device, mesh=mesh, in_specs=in_specs, out_specs=split, check_vma=False
    )
```
